128 devices in a mesh: ctx: 32 (over y, z, core), tp: 4 (over x).
Axes of the slice: x: 4, y: 4, z: 4, core: 2. Of those that a mesh axis runs over, the one named last changes fastest.
Arguments:
- tokens: bfloat16 [4096, 4096], P('ctx', 'tp'), may hold values from -6 to 6
- out_grad: bfloat16 [4096, 4096], P('ctx', 'tp'), may hold values from -4 to 4
- router_probs: bfloat16 [4096, 8], P('ctx'), may hold values from 0.049804688 to 0.5
- expert_ids: int32 [4096, 8], P('ctx'), may hold values from 0 to 63, all different within a row; in each aligned block of 128 rows (0 to 127, 128 to 255, ...) at most 24 rows name the same one
- w_gate: bfloat16 [64, 4096, 1536], P('ctx', None, 'tp'), may hold values from -0.09375 to 0.09375
- w_up: bfloat16 [64, 4096, 1536], P('ctx', None, 'tp'), may hold values from -0.09375 to 0.09375
- w_down: bfloat16 [64, 1536, 4096], P('ctx', 'tp'), may hold values from -0.15625 to 0.15625
Outputs:
- token_grad: bfloat16 [4096, 4096], P('ctx', 'tp')
- prob_grad: bfloat16 [4096, 8], P('ctx')
The draws below stay inside these ranges and needn't reach their ends.
Inputs may be any that keep to these rules, and one draw needn't show every extreme that they name: `expert_ids`: each token names 8 different experts; among the 128 tokens of one index of ctx no expert is named by more than 24 tokens, a bound that some block reaches.
All inputs are finite; a program needn't handle non-finite values.
Results may differ from the reference program's by a relative error of at most 0.015.
Values may be sent and summed in bfloat16 or wider, within the bound.
A program may use at most 128 MiB of HBM per device.

```python
import math
import jax
import jax.numpy as jnp
import numpy as np
from jax import lax

D = 4096
FF = 1536
TOP = 8
TOK_CTX = 128
EXPERTS = 64
CAP = 24
TOKENS = 4096
N_CTX = 32
N_TP = 4


def block_scale(own_key, shape, pieces, least, largest):
    loudness = 1.0
    for axis_at, blocks in pieces:
        heights = jax.random.uniform(jax.random.fold_in(jax.random.fold_in(own_key, 6), axis_at), (blocks,), jnp.float32, least / len(pieces), largest / len(pieces))
        loudness = loudness * jnp.repeat(jnp.exp(heights), shape[axis_at] // blocks).reshape((-1,) + (1,) * (len(shape) - 1 - axis_at))
    return loudness


def assign_block(key, own, number, rows, count, top, most, skew):
    ranking = jax.random.permutation(key, count)
    heavy_load, usual = portions_of(count, rows * top, most, skew, True), portions_of(count, rows * top, most, skew, False)
    places = jnp.arange(count)

    def named(sizes, turn):
        used = int((sizes > 0).sum())
        fixed = max(1, used // 4)
        shifted = fixed + (places - fixed + turn * (used - fixed)) % max(1, count - fixed)
        return jnp.zeros((count,), jnp.int32).at[ranking[jnp.where(places < fixed, places, shifted)]].set(jnp.asarray(sizes, jnp.int32))

    sizes = jnp.where(number % 4 == 0, named(heavy_load, number // 4), named(usual, number - number // 4 - 1))
    mixed = jax.random.permutation(jax.random.fold_in(own, 3), count)
    source_of, receiver = mixed[0:count // 2 * 2:2], mixed[1:count // 2 * 2:2]
    margin = jnp.minimum(sizes[source_of] - 1, most - sizes[receiver]) // 2
    margin = jnp.where((source_of == ranking[0]) | (receiver == ranking[0]) | (sizes[receiver] == 0), 0, jnp.maximum(margin, 0))
    shifted = jax.random.randint(jax.random.fold_in(own, 4), (count // 2,), 0, 1 << 20) % (margin + 1)
    sizes = sizes.at[source_of].add(-shifted).at[receiver].add(shifted)
    members = jnp.searchsorted(jnp.cumsum(sizes), jnp.arange(rows * top), side="right").astype(jnp.int32)
    listing = members.reshape(top, rows).T
    listing = listing[jax.random.permutation(jax.random.fold_in(own, 1), rows)]
    turn = jax.random.randint(jax.random.fold_in(own, 2), (rows, 1), 0, top)
    return jnp.take_along_axis(listing, (jnp.arange(top)[None, :] + turn) % top, axis=1)


def portions_of(number_of, total, most, skew, full):
    weights = [(1 << 20) // math.isqrt(grade ** skew) + 1 for grade in range(1, number_of + 1)]
    largest = most if full else min(most, max(-(-total // number_of), total * weights[0] // sum(weights)))
    least = 1 if total - largest >= number_of - 1 else 0
    given, surplus = [largest] + [least] * (number_of - 1), total - largest - least * (number_of - 1)
    while surplus > 0:
        candidates = [i for i in range(1, number_of) if given[i] < largest] or [i for i in range(1, number_of) if given[i] < most]
        mass, remaining = sum([weights[i] for i in candidates]), surplus
        for i in candidates:
            extra = min(most - given[i], max(1, remaining * weights[i] // mass), surplus)
            given[i] = given[i] + extra
            surplus = surplus - extra
    return np.array(given)


def gaussian(rng, extent, spread, most, split=(), held_as=jnp.bfloat16):
    entries = spread * jax.random.normal(rng, extent, jnp.float32)
    if split:
        entries = entries * block_scale(rng, extent, split, -0.22, 0.18)
    return jnp.clip(entries, -most, most).astype(held_as)


def setup_inputs(seed: int = 0) -> dict:
    seeds = jax.random.split(jax.random.key(seed), 8)
    tokens = gaussian(seeds[0], (TOKENS, D), 1.0, 6.0, ((0, 32), (1, 4)))
    out_grad = gaussian(seeds[1], (TOKENS, D), 0.25, 4.0, ((0, 32), (1, 4)))
    router_probs = jnp.clip(jnp.exp(math.log(0.5) - 2.306499 * jax.random.uniform(seeds[2], (TOKENS, TOP), jnp.float32) ** block_scale(seeds[2], (TOKENS, TOP), ((0, 32),), -0.2, 0.2)), 0.049804688, 0.5).astype(jnp.bfloat16)
    expert_ids_keys = jax.random.split(jax.random.fold_in(seeds[3], 1), TOKENS // TOK_CTX)
    expert_ids_turns = jax.random.permutation(jax.random.fold_in(seeds[3], 3), TOKENS // TOK_CTX)
    expert_ids = jax.vmap(lambda own, number: assign_block(jax.random.fold_in(seeds[3], 2), own, number, TOK_CTX, EXPERTS, TOP, CAP, 2))(expert_ids_keys, expert_ids_turns).reshape((TOKENS, TOP))
    w_gate = gaussian(seeds[4], (EXPERTS, D, FF), D ** -0.5, 0.09375, ((0, 32), (2, 4)))
    w_up = gaussian(seeds[5], (EXPERTS, D, FF), D ** -0.5, 0.09375, ((0, 32), (2, 4)))
    w_down = gaussian(seeds[6], (EXPERTS, FF, D), FF ** -0.5, 0.15625, ((0, 32), (1, 4)))
    return dict(tokens=tokens, out_grad=out_grad, router_probs=router_probs, expert_ids=expert_ids, w_gate=w_gate, w_up=w_up, w_down=w_down)


def expert_pass(operands):
    rows_in, grads_in, weights_in, gate_w, up_w, down_w = operands
    gate_sum = jnp.dot(rows_in, gate_w, preferred_element_type=jnp.float32)
    up_sum = jnp.dot(rows_in, up_w, preferred_element_type=jnp.float32)
    down_back = jnp.dot(grads_in, down_w.T, preferred_element_type=jnp.float32)
    sigmoid_gate = jax.nn.sigmoid(gate_sum)
    gated = gate_sum * sigmoid_gate
    hidden = gated * up_sum
    prob_rows = jnp.sum(hidden * down_back, axis=1).astype(jnp.bfloat16)
    hidden_grad = weights_in.astype(jnp.float32)[:, None] * down_back
    gate_grad = (hidden_grad * up_sum * sigmoid_gate * (1.0 + gate_sum * (1.0 - sigmoid_gate))).astype(jnp.bfloat16)
    up_grad = (hidden_grad * gated).astype(jnp.bfloat16)
    count = rows_in.shape[0]
    shard_width = FF // N_TP
    gate_parts = gate_grad.astype(jnp.float32).reshape(count, N_TP, shard_width)
    up_parts = up_grad.astype(jnp.float32).reshape(count, N_TP, shard_width)
    gate_cols = gate_w.astype(jnp.float32).reshape(D, N_TP, shard_width)
    up_cols = up_w.astype(jnp.float32).reshape(D, N_TP, shard_width)
    partial_value = jnp.einsum("rsf,dsf->rsd", gate_parts, gate_cols, precision=lax.Precision.HIGHEST)
    partial_value = partial_value + jnp.einsum("rsf,dsf->rsd", up_parts, up_cols, precision=lax.Precision.HIGHEST)
    rounded = lax.optimization_barrier(partial_value.astype(jnp.bfloat16))
    row_grads = jnp.sum(rounded.astype(jnp.float32), axis=1).astype(jnp.bfloat16)
    return row_grads, prob_rows


def reference(tokens, out_grad, router_probs, expert_ids, w_gate, w_up, w_down):
    pair_ids = expert_ids.reshape(N_CTX, TOK_CTX * TOP)
    onehot = (pair_ids[:, :, None] == jnp.arange(EXPERTS, dtype=jnp.int32)[None, None, :]).astype(jnp.int32)
    earlier = jnp.cumsum(onehot, axis=1) - onehot
    slot_index = jnp.sum(earlier * onehot, axis=2)
    source = jnp.arange(N_CTX, dtype=jnp.int32)[:, None]
    row_index = (pair_ids * (N_CTX * CAP) + source * CAP + slot_index).reshape(TOKENS * TOP).astype(jnp.int32)
    buffer_rows = EXPERTS * N_CTX * CAP
    token_of = jnp.repeat(jnp.arange(TOKENS, dtype=jnp.int32), TOP)
    x_rows = jnp.zeros((buffer_rows, D), jnp.bfloat16).at[row_index].set(tokens[token_of])
    dy_rows = jnp.zeros((buffer_rows, D), jnp.bfloat16).at[row_index].set(out_grad[token_of])
    p_rows = jnp.zeros((buffer_rows,), jnp.bfloat16).at[row_index].set(router_probs.reshape(TOKENS * TOP))
    per_expert = N_CTX * CAP
    row_grads, prob_rows = lax.map(expert_pass, (x_rows.reshape(EXPERTS, per_expert, D), dy_rows.reshape(EXPERTS, per_expert, D), p_rows.reshape(EXPERTS, per_expert), w_gate, w_up, w_down))
    flat_grads = row_grads.reshape(buffer_rows, D)
    flat_probs = prob_rows.reshape(buffer_rows)
    picked = flat_grads[row_index].reshape(TOKENS, TOP, D)
    token_grad = jnp.sum(picked.astype(jnp.float32), axis=1).astype(jnp.bfloat16)
    prob_grad = flat_probs[row_index].reshape(TOKENS, TOP)
    return token_grad, prob_grad
```

```python
import functools
import jax
import jax.numpy as jnp
from jax import lax
from jax.experimental import pallas as pl
from jax.experimental.pallas import tpu as pltpu
from jax.sharding import PartitionSpec as P

MESH = pl.DeviceIdType.MESH
ORDERS = (("x", "y", "z"), ("y", "z", "x"), ("z", "x", "y"))
SPLITS = (((0, 40), (40, 40), (80, 48)), ((0, 48), (48, 40), (88, 40)))


def my_place():
    ctx = lax.axis_index("ctx")
    return {"x": lax.axis_index("tp"), "y": ctx // 8, "z": (ctx // 2) % 4}, ctx % 2


def device_of(pos, core):
    return ((pos["y"] * 4 + pos["z"]) * 2 + core, pos["x"])


def shifted(pos, axis, by):
    other = dict(pos)
    other[axis] = (pos[axis] + by) % 4
    return other


def entry_barrier(pos, core):
    barrier = pltpu.get_barrier_semaphore()
    for axis in "xyz":
        for by in (1, 3):
            pl.semaphore_signal(barrier, inc=1, device_id=device_of(shifted(pos, axis, by), core), device_id_type=MESH)
    pl.semaphore_signal(barrier, inc=1, device_id=device_of(pos, 1 - core), device_id_type=MESH)
    pl.semaphore_wait(barrier, 7)


def gather_kernel(tok_ref, dy_ref, gx_ref, gy_ref, send, recv, local):
    pos, core = my_place()
    entry_barrier(pos, core)
    width = tok_ref.shape[1]
    own = []
    for t, (src, dst) in enumerate(((tok_ref, gx_ref), (dy_ref, gy_ref))):
        copy = pltpu.make_async_copy(src, dst.at[pos["y"], pos["z"], core, pos["x"]], local.at[t])
        copy.start()
        own.append(copy)
    started = []

    def program(t, color):
        src, dst = ((tok_ref, gx_ref), (dy_ref, gy_ref))[t]
        a, b, c = ORDERS[color]
        r0, rn = SPLITS[t][color]
        rows = pl.ds(r0, rn)

        def slot(at, whole, part=None):
            index = {k: (slice(None) if k in whole else at[k]) for k in "xyz"}
            some = rows
            if part is not None and whole:
                index[a] = pl.ds(2 * part, 2)
            elif part is not None:
                some = pl.ds(r0, 24) if part == 0 else pl.ds(r0 + 24, rn - 24)
            return dst.at[index["y"], index["z"], core, index["x"], some]

        def go(i, source, target, device):
            copy = pltpu.make_async_remote_copy(
                src_ref=source, dst_ref=target, send_sem=send.at[t, color, i],
                recv_sem=recv.at[t, color, i], device_id=device, device_id_type=MESH)
            copy.start()
            started.append(copy)
            return copy

        def block_out(i, at, whole, axis, source=None):
            here = slot(at, whole)
            from_ref = here if source is None else source
            return (go(i, from_ref, here, device_of(shifted(pos, axis, 1), core)),
                    go(i + 1, from_ref, here, device_of(shifted(pos, axis, 3), core)))

        def relay(i, at, whole, axis, pair):
            pair[0].wait_recv()
            piece = slot(shifted(at, axis, 3), whole, 0)
            one = go(i + 2, piece, piece, device_of(shifted(pos, axis, 1), core))
            pair[1].wait_recv()
            piece = slot(shifted(at, axis, 1), whole, 1)
            two = go(i + 3, piece, piece, device_of(shifted(pos, axis, 3), core))
            return one, two

        sib_count = [0]
        sibs = []

        def sibling(at):
            piece = slot(at, (a,))
            sibs.append(go(24 + sib_count[0], piece, piece, device_of(pos, 1 - core)))
            sib_count[0] += 1

        pair = block_out(0, pos, (), a, src.at[rows, :])
        yield
        far = relay(0, pos, (), a, pair)
        yield
        for f in far:
            f.wait_recv()
        if own[t] is not None:
            own[t].wait()
            own[t] = None
        pair = block_out(4, pos, (a,), b)
        lasts = [(8, pos, block_out(8, pos, (a,), c))]
        sibling(pos)
        yield
        far = relay(4, pos, (a,), b, pair)
        for n, by in ((12, 3), (16, 1)):
            at = shifted(pos, b, by)
            lasts.append((n, at, block_out(n, at, (a,), c)))
            sibling(at)
        yield
        for f in far:
            f.wait_recv()
        at = shifted(pos, b, 2)
        lasts.append((20, at, block_out(20, at, (a,), c)))
        sibling(at)
        fars = []
        for n, at, pair in lasts:
            yield
            fars.append((at, relay(n, at, (a,), c, pair)))
            sibling(shifted(at, c, 3))
            sibling(shifted(at, c, 1))
            if len(fars) > 1:
                at2, far = fars[-2]
                for f in far:
                    f.wait_recv()
                sibling(shifted(at2, c, 2))
        yield
        at2, far = fars[-1]
        for f in far:
            f.wait_recv()
        sibling(shifted(at2, c, 2))
        yield
        for s in sibs:
            s.wait_recv()

    LAG = 4
    running = [(0, program(0, col)) for col in range(3)] + [(LAG, program(1, col)) for col in range(3)]
    tick = 0
    live = list(running)
    while live:
        still = []
        for first, prog in live:
            if tick < first:
                still.append((first, prog))
                continue
            try:
                next(prog)
                still.append((first, prog))
            except StopIteration:
                pass
        live = still
        tick += 1
    for s in started:
        s.wait_send()


def gather_all(tokens, out_grad):
    rows, width = tokens.shape
    shape = jax.ShapeDtypeStruct((4, 4, 2, 4, rows, width), tokens.dtype)
    return pl.pallas_call(
        gather_kernel,
        out_shape=(shape, shape),
        in_specs=[pl.BlockSpec(memory_space=pltpu.VMEM)] * 2,
        out_specs=[pl.BlockSpec(memory_space=pl.ANY)] * 2,
        scratch_shapes=[
            pltpu.SemaphoreType.DMA((2, 3, 40)),
            pltpu.SemaphoreType.DMA((2, 3, 40)),
            pltpu.SemaphoreType.DMA((2,)),
        ],
        compiler_params=pltpu.CompilerParams(collective_id=0, has_side_effects=True),
    )(tokens, out_grad)

CAPS = 24


def pair_selectors(ids, probs, first):
    groups, top, toks = ids.shape
    before = (lax.broadcasted_iota(jnp.int32, (toks, toks), 0) < lax.broadcasted_iota(jnp.int32, (toks, toks), 1)).astype(jnp.bfloat16)
    out = []
    for e in range(2):
        masks, hits, slots, weights = [], [], [], []
        for g in range(2):
            mask = (ids[g] == first + e).astype(jnp.float32)
            hit = jnp.sum(mask, axis=0, keepdims=True)
            slot = jnp.dot(jnp.broadcast_to(hit, (8, toks)).astype(jnp.bfloat16), before, preferred_element_type=jnp.float32)[0:1]
            masks.append(mask)
            hits.append(hit)
            slots.append(slot + float(CAPS * g))
            weights.append(jnp.sum(mask * probs[g], axis=0, keepdims=True))
        hit = jnp.concatenate(hits, axis=1)
        slot = jnp.concatenate(slots, axis=1)
        weight = jnp.concatenate(weights, axis=1)
        row = lax.broadcasted_iota(jnp.int32, (2 * CAPS, 2 * toks), 0)
        sel = jnp.where((row == slot.astype(jnp.int32)) & (hit > 0.5), 1.0, 0.0)
        out.append((sel, weight, masks))
    return out


def expert_kernel(ids_ref, probs_ref, x_ref, dy_ref, wg_ref, wu_ref, wd_ref, out_ref, pg_ref,
                  xr, dr, rp, pw, pr, *, sets, per_set):
    step = pl.program_id(0)
    first = lax.axis_index("ctx") * 2
    steps = sets * per_set
    width = x_ref.shape[3]
    quarters = x_ref.shape[1]
    toks = x_ref.shape[2]

    @pl.when(step >= per_set)
    def _():
        i = step - per_set
        at = pl.multiple_of(lax.rem(i, per_set) * 2 * CAPS, 16)
        pair = pl.ds(2 * i, 2)
        chosen = pair_selectors(ids_ref[pair], probs_ref[pair], first)
        both = jnp.concatenate([c[0] for c in chosen], axis=0).astype(jnp.bfloat16)
        for q in range(quarters):
            cols = pl.ds(q * width, width)
            rows = jnp.concatenate([rp[e, pl.ds(at, 2 * CAPS), cols] for e in range(2)], axis=0)
            dense = lax.dot_general(both, rows, (((0,), (0,)), ((), ())), preferred_element_type=jnp.float32)
            dense = dense.astype(jnp.bfloat16)
            for g in range(2):
                out_ref[g, q] = dense[g * toks:(g + 1) * toks]
        total = [0.0, 0.0]
        for e in range(2):
            sel, _w, masks = chosen[e]
            value = jnp.sum(sel * pr[e, pl.ds(at, 2 * CAPS), 0:1], axis=0, keepdims=True)
            for g in range(2):
                total[g] = total[g] + masks[g] * value[:, g * toks:(g + 1) * toks]
        for g in range(2):
            pg_ref[g] = total[g]

    @pl.when(step < steps)
    def _():
        at = pl.multiple_of(lax.rem(step, per_set) * 2 * CAPS, 16)
        pair = pl.ds(2 * step, 2)
        chosen = pair_selectors(ids_ref[pair], probs_ref[pair], first)
        both = jnp.concatenate([c[0] for c in chosen], axis=0).astype(jnp.bfloat16)
        for src, dst in ((x_ref, xr), (dy_ref, dr)):
            for q in range(quarters):
                two = src[:, q].reshape(2 * toks, width)
                rows = jnp.dot(both, two, preferred_element_type=jnp.float32).astype(jnp.bfloat16)
                for e in range(2):
                    dst[e, pl.ds(at, 2 * CAPS), pl.ds(q * width, width)] = rows[e * 2 * CAPS:(e + 1) * 2 * CAPS]
        for e in range(2):
            sel, weight, _m = chosen[e]
            col = jnp.sum(sel * weight, axis=1, keepdims=True)
            pw[e, pl.ds(at, 2 * CAPS), :] = jnp.broadcast_to(col, (2 * CAPS, 128))

    @pl.when((step < steps) & (lax.rem(step, per_set) == per_set - 1))
    def _():
        for e in range(2):
            gate = jnp.dot(xr[e], wg_ref[e], preferred_element_type=jnp.float32)
            up = jnp.dot(xr[e], wu_ref[e], preferred_element_type=jnp.float32)
            back = lax.dot_general(dr[e], wd_ref[e], (((1,), (1,)), ((), ())), preferred_element_type=jnp.float32)
            sig = jax.nn.sigmoid(gate)
            gated = gate * sig
            pr[e] = jnp.broadcast_to(jnp.sum(gated * up * back, axis=1, keepdims=True), pr.shape[1:])
            scaled = pw[e, :, 0:1] * back
            gg = (scaled * up * sig * (1.0 + gate * (1.0 - sig))).astype(jnp.bfloat16)
            ug = (scaled * gated).astype(jnp.bfloat16)
            dims = (((1,), (1,)), ((), ()))
            depth = wg_ref.shape[1]
            block = 1024
            for d in range(depth // block):
                cols = pl.ds(d * block, block)
                part = lax.dot_general(gg, wg_ref[e, cols, :], dims, preferred_element_type=jnp.float32)
                part = part + lax.dot_general(ug, wu_ref[e, cols, :], dims, preferred_element_type=jnp.float32)
                rp[e, :, cols] = part.astype(jnp.bfloat16)


def expert_pass(ids, probs, gx, gy, wg, wu, wd):
    groups, quarters, toks, width = gx.shape
    depth, ff = wg.shape[1:]
    per_set = 4
    sets = groups // 2 // per_set
    steps = sets * per_set
    rows = per_set * 2 * CAPS
    one = pl.Buffered(1)
    zero3 = lambda i: (0, 0, 0)
    return pl.pallas_call(
        functools.partial(expert_kernel, sets=sets, per_set=per_set),
        grid=(steps + per_set,),
        out_shape=(jax.ShapeDtypeStruct(gx.shape, jnp.bfloat16), jax.ShapeDtypeStruct((groups,) + ids.shape[1:], jnp.float32)),
        in_specs=[
            pl.BlockSpec(ids.shape, zero3),
            pl.BlockSpec(probs.shape, zero3),
            pl.BlockSpec((2, quarters, toks, width), lambda i: (jnp.minimum(i, steps - 1), 0, 0, 0)),
            pl.BlockSpec((2, quarters, toks, width), lambda i: (jnp.minimum(i, steps - 1), 0, 0, 0)),
            pl.BlockSpec(wg.shape, zero3, pipeline_mode=one),
            pl.BlockSpec(wu.shape, zero3, pipeline_mode=one),
            pl.BlockSpec(wd.shape, zero3, pipeline_mode=one),
        ],
        out_specs=[
            pl.BlockSpec((2, quarters, toks, width), lambda i: (jnp.maximum(i - per_set, 0), 0, 0, 0)),
            pl.BlockSpec((2,) + ids.shape[1:], lambda i: (jnp.maximum(i - per_set, 0), 0, 0)),
        ],
        scratch_shapes=[
            pltpu.VMEM((2, rows, depth), jnp.bfloat16),
            pltpu.VMEM((2, rows, depth), jnp.bfloat16),
            pltpu.VMEM((2, rows, depth), jnp.bfloat16),
            pltpu.VMEM((2, rows, 128), jnp.float32),
            pltpu.VMEM((2, rows, 128), jnp.float32),
        ],
        compiler_params=pltpu.CompilerParams(vmem_limit_bytes=60 * 1024 * 1024),
    )(ids, probs, gx, gy, wg, wu, wd)

PARTS = ((0, 48), (48, 48), (96, 32))


def scatter_kernel(p_ref, out_ref, *scratch):
    accs, sibs, fulls, parts, lone_full, lone_part = (scratch[3 * i:3 * i + 3] for i in range(6))
    send, recv, local = scratch[18:]
    pos, core = my_place()
    entry_barrier(pos, core)
    width = out_ref.shape[1]
    half = width // 2
    cuts = (pl.ds(0, half), pl.ds(half, half))
    started = []

    def go(color, i, source, target, device):
        copy = pltpu.make_async_remote_copy(
            src_ref=source, dst_ref=target, send_sem=send.at[color, i],
            recv_sem=recv.at[color, i], device_id=device, device_id_type=MESH)
        copy.start()
        started.append(copy)
        return copy

    def program(color):
        a, b, c = ORDERS[color]
        rows = pl.ds(*PARTS[color])
        acc, sib = accs[color], sibs[color]

        def where(at, whole):
            index = {k: (slice(None) if k in whole else at[k]) for k in "xyz"}
            return index["y"], index["z"], index["x"]

        def line(at, part=None):
            index = dict(zip("yzx", where(at, (a,))))
            if part is not None:
                index[a] = pl.ds(2 * part, 2)
            return acc.at[index["y"], index["z"], index["x"]]

        def add_line(at, part, other):
            low, high = (0, 4) if part is None else (2 * part, 2 * part + 2)

            def body(i, carry):
                mine = dict(at)
                mine[a] = i
                spot = where(mine, ())
                acc[spot] = acc[spot] + other(i - low)
                return carry
            lax.fori_loop(low, high, body, 0)

        loads = {}
        order = (2, 1, 3, 0)
        count = 0
        for j in order:
            for k in order:
                at = shifted(shifted(pos, b, j), c, k)
                y, z, x = where(at, (a,))
                load = pltpu.make_async_copy(p_ref.at[y, z, core, x, rows], line(at), local.at[color, count])
                load.start()
                push = go(color, 24 + count, p_ref.at[y, z, 1 - core, x, rows], sib.at[y, z, x], device_of(pos, 1 - core))
                loads[j, k] = (at, load, push)
                count += 1
            yield

        def merge(j, k):
            at, load, push = loads[j, k]
            load.wait()
            push.wait_recv()

            def other(i):
                mine = dict(at)
                mine[a] = i
                return sib[where(mine, ())]
            add_line(at, None, other)

        def first(n, axis, unit):
            return (go(color, n * 4, unit(2, 0), parts[color].at[n, 0], device_of(shifted(pos, axis, 1), core)),
                    go(color, n * 4 + 1, unit(2, 1), parts[color].at[n, 1], device_of(shifted(pos, axis, 3), core)))

        def second(n, axis, unit, add, halves):
            sent = []
            for side, by in ((0, 1), (1, 3)):
                halves[side].wait_recv()
                add(by, side, lambda i, side=side: parts[color][n, side, i])
                sent.append(go(color, n * 4 + 2 + side, unit(by, None), fulls[color].at[n, side],
                               device_of(shifted(pos, axis, by), core)))
            return sent

        def third(n, add, sent):
            for side in range(2):
                sent[side].wait_recv()
                add(0, None, lambda i, side=side: fulls[color][n, side, i])

        def last_unit(j):
            return (lambda k, cols: line(shifted(shifted(pos, b, j), c, k), cols),
                    lambda k, cols, other: add_line(shifted(shifted(pos, b, j), c, k), cols, other))

        halves, sents = {}, {}

        def stage_a(n):
            merge(order[n], 2)
            halves[n] = first(n, c, last_unit(order[n])[0])

        def stage_b(n):
            merge(order[n], 1)
            merge(order[n], 3)
            unit, add = last_unit(order[n])
            sents[n] = second(n, c, unit, add, halves[n])

        def stage_c(n):
            merge(order[n], 0)
            third(n, last_unit(order[n])[1], sents[n])

        mid_unit = lambda k, cols: line(shifted(pos, b, k), cols)
        mid_add = lambda k, cols, other: add_line(shifted(pos, b, k), cols, other)
        stage_a(0)
        yield
        stage_a(1)
        yield
        stage_b(0)
        yield
        stage_a(2)
        yield
        stage_b(1)
        yield
        stage_c(0)
        mid_halves = first(4, b, mid_unit)
        yield
        stage_a(3)
        yield
        stage_b(2)
        yield
        stage_c(1)
        yield
        stage_b(3)
        yield
        stage_c(2)
        mid_sent = second(4, b, mid_unit, mid_add, mid_halves)
        yield
        stage_c(3)
        third(4, mid_add, mid_sent)
        yield

        def one(at, cols=slice(None)):
            return acc.at[(*where(at, ()), slice(None), cols)]

        def add_one(by, cols, other):
            spot = (*where(shifted(pos, a, by), ()), slice(None), cols)
            acc[spot] = acc[spot] + other

        tail = [go(color, 20, one(shifted(pos, a, 2), cuts[0]), lone_part[color].at[0], device_of(shifted(pos, a, 1), core)),
                go(color, 21, one(shifted(pos, a, 2), cuts[1]), lone_part[color].at[1], device_of(shifted(pos, a, 3), core))]
        yield
        sent = []
        for side, by in ((0, 1), (1, 3)):
            tail[side].wait_recv()
            add_one(by, cuts[side], lone_part[color][side])
            sent.append(go(color, 22 + side, one(shifted(pos, a, by)), lone_full[color].at[side], device_of(shifted(pos, a, by), core)))
        yield
        for side in range(2):
            sent[side].wait_recv()
            add_one(0, slice(None), lone_full[color][side])
        out_ref[rows, :] = acc[where(pos, ())]

    live = [program(color) for color in range(3)]
    while live:
        still = []
        for prog in live:
            try:
                next(prog)
                still.append(prog)
            except StopIteration:
                pass
        live = still
    for s in started:
        s.wait_send()


def scatter_all(dense):
    rows, width = dense.shape[-2:]
    half = width // 2
    bf = jnp.bfloat16
    scratch = []
    for make in (
        lambda n: (4, 4, 4, n, width),
        lambda n: (4, 4, 4, n, width),
        lambda n: (5, 2, 4, n, width),
        lambda n: (5, 2, 2, n, width),
        lambda n: (2, n, width),
        lambda n: (2, n, half),
    ):
        scratch += [pltpu.VMEM(make(n), bf) for _, n in PARTS]
    return pl.pallas_call(
        scatter_kernel,
        out_shape=jax.ShapeDtypeStruct((rows, width), bf),
        in_specs=[pl.BlockSpec(memory_space=pl.ANY)],
        out_specs=pl.BlockSpec(memory_space=pltpu.VMEM),
        scratch_shapes=scratch + [
            pltpu.SemaphoreType.DMA((3, 40)),
            pltpu.SemaphoreType.DMA((3, 40)),
            pltpu.SemaphoreType.DMA((3, 16)),
        ],
        compiler_params=pltpu.CompilerParams(collective_id=1, has_side_effects=True, vmem_limit_bytes=62 * 1024 * 1024),
    )(dense)


def on_device(tokens, out_grad, router_probs, expert_ids, w_gate, w_up, w_down):
    toks, width = tokens.shape
    gx, gy = gather_all(tokens, out_grad)
    ids = lax.all_gather(expert_ids.T, "ctx", axis=0)
    probs = lax.all_gather(router_probs.T, "ctx", axis=0).astype(jnp.float32)
    flat = (32, 4, toks, width)
    dense, pg = expert_pass(ids, probs, gx.reshape(flat), gy.reshape(flat), w_gate, w_up, w_down)
    token_grad = scatter_all(dense.reshape(gx.shape))
    pg = lax.psum_scatter(pg, "ctx", scatter_dimension=0, tiled=True)
    pg = lax.psum(pg, "tp")
    return token_grad, pg[0].T.astype(jnp.bfloat16)


def solution(mesh):
    return jax.shard_map(
        on_device,
        mesh=mesh,
        in_specs=(P("ctx", "tp"), P("ctx", "tp"), P("ctx", None), P("ctx", None), P("ctx", None, "tp"), P("ctx", None, "tp"), P("ctx", "tp", None)),
        out_specs=(P("ctx", "tp"), P("ctx", None)),
        check_vma=False,
    )
```

```python
import functools
import jax
import jax.numpy as jnp
from jax import lax
from jax.experimental import pallas as pl
from jax.experimental.pallas import tpu as pltpu
from jax.sharding import PartitionSpec as P

MESH = pl.DeviceIdType.MESH
ORDERS = (("x", "y", "z"), ("y", "z", "x"), ("z", "x", "y"))
SPLITS = (((0, 40), (40, 40), (80, 48)), ((0, 48), (48, 40), (88, 40)))


def my_place():
    ctx = lax.axis_index("ctx")
    return {"x": lax.axis_index("tp"), "y": ctx // 8, "z": (ctx // 2) % 4}, ctx % 2


def device_of(pos, core):
    return ((pos["y"] * 4 + pos["z"]) * 2 + core, pos["x"])


def shifted(pos, axis, by):
    other = dict(pos)
    other[axis] = (pos[axis] + by) % 4
    return other


def entry_barrier(pos, core):
    barrier = pltpu.get_barrier_semaphore()
    for axis in "xyz":
        for by in (1, 3):
            pl.semaphore_signal(barrier, inc=1, device_id=device_of(shifted(pos, axis, by), core), device_id_type=MESH)
    pl.semaphore_signal(barrier, inc=1, device_id=device_of(pos, 1 - core), device_id_type=MESH)
    pl.semaphore_wait(barrier, 7)


def gather_kernel(tok_ref, dy_ref, meta_ref, gx_ref, gy_ref, gm_ref, send, recv, msend, mrecv, local):
    pos, core = my_place()
    entry_barrier(pos, core)
    width = tok_ref.shape[1]
    own = []
    for t, (src, dst) in enumerate(((tok_ref, gx_ref), (dy_ref, gy_ref))):
        copy = pltpu.make_async_copy(src, dst.at[pos["y"], pos["z"], core, pos["x"]], local.at[t])
        copy.start()
        own.append(copy)
    own_meta = pltpu.make_async_copy(meta_ref, gm_ref.at[pos["y"], pos["z"], core], local.at[2])
    own_meta.start()
    started = []

    def meta_program():
        def go(i, source, target, device):
            copy = pltpu.make_async_remote_copy(
                src_ref=source, dst_ref=target, send_sem=msend.at[i], recv_sem=mrecv.at[i],
                device_id=device, device_id_type=MESH)
            copy.start()
            started.append(copy)
            return copy

        here = gm_ref.at[pos["y"], pos["z"], core]
        one = go(0, meta_ref, here, device_of(shifted(pos, "y", 1), core))
        two = go(1, meta_ref, here, device_of(shifted(pos, "y", 3), core))
        yield
        one.wait_recv()
        back = gm_ref.at[shifted(pos, "y", 3)["y"], pos["z"], core]
        far = go(2, back, back, device_of(shifted(pos, "y", 1), core))
        two.wait_recv()
        yield
        far.wait_recv()
        own_meta.wait()
        here = gm_ref.at[:, pos["z"], core]
        one = go(3, here, here, device_of(shifted(pos, "z", 1), core))
        two = go(4, here, here, device_of(shifted(pos, "z", 3), core))
        yield
        one.wait_recv()
        back = gm_ref.at[:, shifted(pos, "z", 3)["z"], core]
        far = go(5, back, back, device_of(shifted(pos, "z", 1), core))
        two.wait_recv()
        yield
        far.wait_recv()
        mine = gm_ref.at[:, :, core]
        last = go(6, mine, mine, device_of(pos, 1 - core))
        yield
        last.wait_recv()

    def program(t, color):
        src, dst = ((tok_ref, gx_ref), (dy_ref, gy_ref))[t]
        a, b, c = ORDERS[color]
        r0, rn = SPLITS[t][color]
        rows = pl.ds(r0, rn)

        def slot(at, whole, part=None):
            index = {k: (slice(None) if k in whole else at[k]) for k in "xyz"}
            some = rows
            if part is not None and whole:
                index[a] = pl.ds(2 * part, 2)
            elif part is not None:
                some = pl.ds(r0, 24) if part == 0 else pl.ds(r0 + 24, rn - 24)
            return dst.at[index["y"], index["z"], core, index["x"], some]

        def go(i, source, target, device):
            copy = pltpu.make_async_remote_copy(
                src_ref=source, dst_ref=target, send_sem=send.at[t, color, i],
                recv_sem=recv.at[t, color, i], device_id=device, device_id_type=MESH)
            copy.start()
            started.append(copy)
            return copy

        def block_out(i, at, whole, axis, source=None):
            here = slot(at, whole)
            from_ref = here if source is None else source
            return (go(i, from_ref, here, device_of(shifted(pos, axis, 1), core)),
                    go(i + 1, from_ref, here, device_of(shifted(pos, axis, 3), core)))

        def relay(i, at, whole, axis, pair):
            pair[0].wait_recv()
            piece = slot(shifted(at, axis, 3), whole, 0)
            one = go(i + 2, piece, piece, device_of(shifted(pos, axis, 1), core))
            pair[1].wait_recv()
            piece = slot(shifted(at, axis, 1), whole, 1)
            two = go(i + 3, piece, piece, device_of(shifted(pos, axis, 3), core))
            return one, two

        sib_count = [0]
        sibs = []

        def sibling(at):
            piece = slot(at, (a,))
            sibs.append(go(24 + sib_count[0], piece, piece, device_of(pos, 1 - core)))
            sib_count[0] += 1

        pair = block_out(0, pos, (), a, src.at[rows, :])
        yield
        far = relay(0, pos, (), a, pair)
        yield
        for f in far:
            f.wait_recv()
        if own[t] is not None:
            own[t].wait()
            own[t] = None
        pair = block_out(4, pos, (a,), b)
        lasts = [(8, pos, block_out(8, pos, (a,), c))]
        sibling(pos)
        yield
        far = relay(4, pos, (a,), b, pair)
        for n, by in ((12, 3), (16, 1)):
            at = shifted(pos, b, by)
            lasts.append((n, at, block_out(n, at, (a,), c)))
            sibling(at)
        yield
        for f in far:
            f.wait_recv()
        at = shifted(pos, b, 2)
        lasts.append((20, at, block_out(20, at, (a,), c)))
        sibling(at)
        fars = []
        for n, at, pair in lasts:
            yield
            fars.append((at, relay(n, at, (a,), c, pair)))
            sibling(shifted(at, c, 3))
            sibling(shifted(at, c, 1))
            if len(fars) > 1:
                at2, far = fars[-2]
                for f in far:
                    f.wait_recv()
                sibling(shifted(at2, c, 2))
        yield
        at2, far = fars[-1]
        for f in far:
            f.wait_recv()
        sibling(shifted(at2, c, 2))
        yield
        for s in sibs:
            s.wait_recv()

    LAG = 4
    running = [(0, meta_program())] + [(0, program(0, col)) for col in range(3)] + [(LAG, program(1, col)) for col in range(3)]
    tick = 0
    live = list(running)
    while live:
        still = []
        for first, prog in live:
            if tick < first:
                still.append((first, prog))
                continue
            try:
                next(prog)
                still.append((first, prog))
            except StopIteration:
                pass
        live = still
        tick += 1
    for s in started:
        s.wait_send()


def gather_all(tokens, out_grad, meta):
    rows, width = tokens.shape
    shape = jax.ShapeDtypeStruct((4, 4, 2, 4, rows, width), tokens.dtype)
    return pl.pallas_call(
        gather_kernel,
        out_shape=(shape, shape, jax.ShapeDtypeStruct((4, 4, 2) + meta.shape, meta.dtype)),
        in_specs=[pl.BlockSpec(memory_space=pltpu.VMEM)] * 3,
        out_specs=[pl.BlockSpec(memory_space=pl.ANY)] * 3,
        scratch_shapes=[
            pltpu.SemaphoreType.DMA((2, 3, 40)),
            pltpu.SemaphoreType.DMA((2, 3, 40)),
            pltpu.SemaphoreType.DMA((8,)),
            pltpu.SemaphoreType.DMA((8,)),
            pltpu.SemaphoreType.DMA((3,)),
        ],
        compiler_params=pltpu.CompilerParams(collective_id=0, has_side_effects=True),
    )(tokens, out_grad, meta)

CAPS = 24


def pair_selectors(meta, first):
    top, toks = meta.shape[1] // 2, meta.shape[2]
    ids, probs = meta[:, :top].astype(jnp.int32), meta[:, top:]
    before = (lax.broadcasted_iota(jnp.int32, (toks, toks), 0) < lax.broadcasted_iota(jnp.int32, (toks, toks), 1)).astype(jnp.bfloat16)
    out = []
    for e in range(2):
        masks, hits, slots, weights = [], [], [], []
        for g in range(2):
            mask = (ids[g] == first + e).astype(jnp.float32)
            hit = jnp.sum(mask, axis=0, keepdims=True)
            slot = jnp.dot(jnp.broadcast_to(hit, (8, toks)).astype(jnp.bfloat16), before, preferred_element_type=jnp.float32)[0:1]
            masks.append(mask)
            hits.append(hit)
            slots.append(slot + float(CAPS * g))
            weights.append(jnp.sum(mask * probs[g], axis=0, keepdims=True))
        hit = jnp.concatenate(hits, axis=1)
        slot = jnp.concatenate(slots, axis=1)
        weight = jnp.concatenate(weights, axis=1)
        row = lax.broadcasted_iota(jnp.int32, (2 * CAPS, 2 * toks), 0)
        sel = jnp.where((row == slot.astype(jnp.int32)) & (hit > 0.5), 1.0, 0.0)
        out.append((sel, weight, masks))
    return out


def expert_kernel(meta_ref, x_ref, dy_ref, wg_ref, wu_ref, wd_ref, out_ref, pg_ref,
                  xr, dr, rp, pw, pr, *, sets, per_set):
    step = pl.program_id(0)
    first = lax.axis_index("ctx") * 2
    steps = sets * per_set
    width = x_ref.shape[3]
    quarters = x_ref.shape[1]
    toks = x_ref.shape[2]

    @pl.when(step >= per_set)
    def _():
        i = step - per_set
        at = pl.multiple_of(lax.rem(i, per_set) * 2 * CAPS, 16)
        pair = pl.ds(2 * i, 2)
        chosen = pair_selectors(meta_ref[pair], first)
        both = jnp.concatenate([c[0] for c in chosen], axis=0).astype(jnp.bfloat16)
        for q in range(quarters):
            cols = pl.ds(q * width, width)
            rows = jnp.concatenate([rp[e, pl.ds(at, 2 * CAPS), cols] for e in range(2)], axis=0)
            dense = lax.dot_general(both, rows, (((0,), (0,)), ((), ())), preferred_element_type=jnp.float32)
            dense = dense.astype(jnp.bfloat16)
            for g in range(2):
                out_ref[g, q] = dense[g * toks:(g + 1) * toks]
        total = [0.0, 0.0]
        for e in range(2):
            sel, _w, masks = chosen[e]
            value = jnp.sum(sel * pr[e, pl.ds(at, 2 * CAPS), 0:1], axis=0, keepdims=True)
            for g in range(2):
                total[g] = total[g] + masks[g] * value[:, g * toks:(g + 1) * toks]
        for g in range(2):
            pg_ref[g] = total[g]

    @pl.when(step < steps)
    def _():
        at = pl.multiple_of(lax.rem(step, per_set) * 2 * CAPS, 16)
        pair = pl.ds(2 * step, 2)
        chosen = pair_selectors(meta_ref[pair], first)
        both = jnp.concatenate([c[0] for c in chosen], axis=0).astype(jnp.bfloat16)
        for src, dst in ((x_ref, xr), (dy_ref, dr)):
            for q in range(quarters):
                two = src[:, q].reshape(2 * toks, width)
                rows = jnp.dot(both, two, preferred_element_type=jnp.float32).astype(jnp.bfloat16)
                for e in range(2):
                    dst[e, pl.ds(at, 2 * CAPS), pl.ds(q * width, width)] = rows[e * 2 * CAPS:(e + 1) * 2 * CAPS]
        for e in range(2):
            sel, weight, _m = chosen[e]
            col = jnp.sum(sel * weight, axis=1, keepdims=True)
            pw[e, pl.ds(at, 2 * CAPS), :] = jnp.broadcast_to(col, (2 * CAPS, 128))

    @pl.when((step < steps) & (lax.rem(step, per_set) == per_set - 1))
    def _():
        for e in range(2):
            gate = jnp.dot(xr[e], wg_ref[e], preferred_element_type=jnp.float32)
            up = jnp.dot(xr[e], wu_ref[e], preferred_element_type=jnp.float32)
            back = lax.dot_general(dr[e], wd_ref[e], (((1,), (1,)), ((), ())), preferred_element_type=jnp.float32)
            sig = jax.nn.sigmoid(gate)
            gated = gate * sig
            pr[e] = jnp.broadcast_to(jnp.sum(gated * up * back, axis=1, keepdims=True), pr.shape[1:])
            scaled = pw[e, :, 0:1] * back
            gg = (scaled * up * sig * (1.0 + gate * (1.0 - sig))).astype(jnp.bfloat16)
            ug = (scaled * gated).astype(jnp.bfloat16)
            dims = (((1,), (1,)), ((), ()))
            depth = wg_ref.shape[1]
            block = 1024
            for d in range(depth // block):
                cols = pl.ds(d * block, block)
                part = lax.dot_general(gg, wg_ref[e, cols, :], dims, preferred_element_type=jnp.float32)
                part = part + lax.dot_general(ug, wu_ref[e, cols, :], dims, preferred_element_type=jnp.float32)
                rp[e, :, cols] = part.astype(jnp.bfloat16)


def expert_pass(meta, gx, gy, wg, wu, wd):
    groups, quarters, toks, width = gx.shape
    depth, ff = wg.shape[1:]
    per_set = 4
    sets = groups // 2 // per_set
    steps = sets * per_set
    rows = per_set * 2 * CAPS
    one = pl.Buffered(1)
    zero3 = lambda i: (0, 0, 0)
    return pl.pallas_call(
        functools.partial(expert_kernel, sets=sets, per_set=per_set),
        grid=(steps + per_set,),
        out_shape=(jax.ShapeDtypeStruct(gx.shape, jnp.bfloat16), jax.ShapeDtypeStruct((groups, meta.shape[1] // 2, toks), jnp.float32)),
        in_specs=[
            pl.BlockSpec(meta.shape, zero3),
            pl.BlockSpec((2, quarters, toks, width), lambda i: (jnp.minimum(i, steps - 1), 0, 0, 0)),
            pl.BlockSpec((2, quarters, toks, width), lambda i: (jnp.minimum(i, steps - 1), 0, 0, 0)),
            pl.BlockSpec(wg.shape, zero3, pipeline_mode=one),
            pl.BlockSpec(wu.shape, zero3, pipeline_mode=one),
            pl.BlockSpec(wd.shape, zero3, pipeline_mode=one),
        ],
        out_specs=[
            pl.BlockSpec((2, quarters, toks, width), lambda i: (jnp.maximum(i - per_set, 0), 0, 0, 0)),
            pl.BlockSpec((2, meta.shape[1] // 2, toks), lambda i: (jnp.maximum(i - per_set, 0), 0, 0)),
        ],
        scratch_shapes=[
            pltpu.VMEM((2, rows, depth), jnp.bfloat16),
            pltpu.VMEM((2, rows, depth), jnp.bfloat16),
            pltpu.VMEM((2, rows, depth), jnp.bfloat16),
            pltpu.VMEM((2, rows, 128), jnp.float32),
            pltpu.VMEM((2, rows, 128), jnp.float32),
        ],
        compiler_params=pltpu.CompilerParams(vmem_limit_bytes=60 * 1024 * 1024),
    )(meta, gx, gy, wg, wu, wd)

PARTS = ((0, 48), (48, 48), (96, 32))


def scatter_kernel(p_ref, pg_ref, out_ref, prob_ref, *scratch):
    accs, sibs, fulls, parts, lone_full, lone_part = (scratch[3 * i:3 * i + 3] for i in range(6))
    pacc, psib, pring, pall, psend, precv, send, recv, local = scratch[18:]
    pos, core = my_place()
    entry_barrier(pos, core)
    width = out_ref.shape[1]
    half = width // 2
    cuts = (pl.ds(0, half), pl.ds(half, half))
    started = []

    def go(color, i, source, target, device):
        copy = pltpu.make_async_remote_copy(
            src_ref=source, dst_ref=target, send_sem=send.at[color, i],
            recv_sem=recv.at[color, i], device_id=device, device_id_type=MESH)
        copy.start()
        started.append(copy)
        return copy

    def prob_program():
        def go(i, source, target, device):
            copy = pltpu.make_async_remote_copy(
                src_ref=source, dst_ref=target, send_sem=psend.at[i], recv_sem=precv.at[i],
                device_id=device, device_id_type=MESH)
            copy.start()
            started.append(copy)
            return copy

        load = pltpu.make_async_copy(pg_ref.at[:, :, core], pacc, local.at[3, 0])
        load.start()
        push = go(0, pg_ref.at[:, :, 1 - core], psib, device_of(pos, 1 - core))
        yield
        load.wait()
        push.wait_recv()
        for i in range(4):
            pacc[i] = pacc[i] + psib[i]
        n = 1
        for stage, axis in enumerate("zy"):
            def spot(by):
                at = shifted(pos, axis, by)
                return (slice(None), at["z"]) if axis == "z" else (pl.ds(at["y"], 1), at["z"])
            size = 4 if axis == "z" else 1
            ring = [pring.at[stage, i, pl.ds(0, size)] for i in range(3)]
            plus, minus = device_of(shifted(pos, axis, 1), core), device_of(shifted(pos, axis, 3), core)
            far = go(n, pacc.at[spot(2)], ring[0], plus)
            yield
            far.wait_recv()
            pacc[spot(1)] = pacc[spot(1)] + ring[0][...]
            one = go(n + 1, pacc.at[spot(1)], ring[1], plus)
            two = go(n + 2, pacc.at[spot(3)], ring[2], minus)
            yield
            one.wait_recv()
            two.wait_recv()
            pacc[spot(0)] = pacc[spot(0)] + ring[1][...] + ring[2][...]
            n += 3
        pall[pos["x"]] = pacc[pos["y"], pos["z"]]
        here = pall.at[pos["x"]]
        one = go(n, here, here, device_of(shifted(pos, "x", 1), core))
        two = go(n + 1, here, here, device_of(shifted(pos, "x", 3), core))
        yield
        one.wait_recv()
        back = pall.at[shifted(pos, "x", 3)["x"]]
        far = go(n + 2, back, back, device_of(shifted(pos, "x", 1), core))
        two.wait_recv()
        yield
        far.wait_recv()
        prob_ref[...] = pall[0] + pall[1] + pall[2] + pall[3]

    def program(color):
        a, b, c = ORDERS[color]
        rows = pl.ds(*PARTS[color])
        acc, sib = accs[color], sibs[color]

        def where(at, whole):
            index = {k: (slice(None) if k in whole else at[k]) for k in "xyz"}
            return index["y"], index["z"], index["x"]

        def line(at, part=None):
            index = dict(zip("yzx", where(at, (a,))))
            if part is not None:
                index[a] = pl.ds(2 * part, 2)
            return acc.at[index["y"], index["z"], index["x"]]

        def add_line(at, part, other):
            low, high = (0, 4) if part is None else (2 * part, 2 * part + 2)

            def body(i, carry):
                mine = dict(at)
                mine[a] = i
                spot = where(mine, ())
                acc[spot] = acc[spot] + other(i - low)
                return carry
            lax.fori_loop(low, high, body, 0)

        loads = {}
        order = (2, 1, 3, 0)
        count = 0
        for j in order:
            for k in order:
                at = shifted(shifted(pos, b, j), c, k)
                y, z, x = where(at, (a,))
                load = pltpu.make_async_copy(p_ref.at[y, z, core, x, rows], line(at), local.at[color, count])
                load.start()
                push = go(color, 24 + count, p_ref.at[y, z, 1 - core, x, rows], sib.at[y, z, x], device_of(pos, 1 - core))
                loads[j, k] = (at, load, push)
                count += 1
            yield

        def merge(j, k):
            at, load, push = loads[j, k]
            load.wait()
            push.wait_recv()

            def other(i):
                mine = dict(at)
                mine[a] = i
                return sib[where(mine, ())]
            add_line(at, None, other)

        def first(n, axis, unit):
            return (go(color, n * 4, unit(2, 0), parts[color].at[n, 0], device_of(shifted(pos, axis, 1), core)),
                    go(color, n * 4 + 1, unit(2, 1), parts[color].at[n, 1], device_of(shifted(pos, axis, 3), core)))

        def second(n, axis, unit, add, halves):
            sent = []
            for side, by in ((0, 1), (1, 3)):
                halves[side].wait_recv()
                add(by, side, lambda i, side=side: parts[color][n, side, i])
                sent.append(go(color, n * 4 + 2 + side, unit(by, None), fulls[color].at[n, side],
                               device_of(shifted(pos, axis, by), core)))
            return sent

        def third(n, add, sent):
            for side in range(2):
                sent[side].wait_recv()
                add(0, None, lambda i, side=side: fulls[color][n, side, i])

        def last_unit(j):
            return (lambda k, cols: line(shifted(shifted(pos, b, j), c, k), cols),
                    lambda k, cols, other: add_line(shifted(shifted(pos, b, j), c, k), cols, other))

        halves, sents = {}, {}

        def stage_a(n):
            merge(order[n], 2)
            halves[n] = first(n, c, last_unit(order[n])[0])

        def stage_b(n):
            merge(order[n], 1)
            merge(order[n], 3)
            unit, add = last_unit(order[n])
            sents[n] = second(n, c, unit, add, halves[n])

        def stage_c(n):
            merge(order[n], 0)
            third(n, last_unit(order[n])[1], sents[n])

        mid_unit = lambda k, cols: line(shifted(pos, b, k), cols)
        mid_add = lambda k, cols, other: add_line(shifted(pos, b, k), cols, other)
        stage_a(0)
        yield
        stage_a(1)
        yield
        stage_b(0)
        yield
        stage_a(2)
        yield
        stage_b(1)
        yield
        stage_c(0)
        mid_halves = first(4, b, mid_unit)
        yield
        stage_a(3)
        yield
        stage_b(2)
        yield
        stage_c(1)
        yield
        stage_b(3)
        yield
        stage_c(2)
        mid_sent = second(4, b, mid_unit, mid_add, mid_halves)
        yield
        stage_c(3)
        third(4, mid_add, mid_sent)
        yield

        def one(at, cols=slice(None)):
            return acc.at[(*where(at, ()), slice(None), cols)]

        def add_one(by, cols, other):
            spot = (*where(shifted(pos, a, by), ()), slice(None), cols)
            acc[spot] = acc[spot] + other

        tail = [go(color, 20, one(shifted(pos, a, 2), cuts[0]), lone_part[color].at[0], device_of(shifted(pos, a, 1), core)),
                go(color, 21, one(shifted(pos, a, 2), cuts[1]), lone_part[color].at[1], device_of(shifted(pos, a, 3), core))]
        yield
        sent = []
        for side, by in ((0, 1), (1, 3)):
            tail[side].wait_recv()
            add_one(by, cuts[side], lone_part[color][side])
            sent.append(go(color, 22 + side, one(shifted(pos, a, by)), lone_full[color].at[side], device_of(shifted(pos, a, by), core)))
        yield
        for side in range(2):
            sent[side].wait_recv()
            add_one(0, slice(None), lone_full[color][side])
        out_ref[rows, :] = acc[where(pos, ())]

    live = [prob_program()] + [program(color) for color in range(3)]
    while live:
        still = []
        for prog in live:
            try:
                next(prog)
                still.append(prog)
            except StopIteration:
                pass
        live = still
    for s in started:
        s.wait_send()


def scatter_all(dense, pg):
    rows, width = dense.shape[-2:]
    half = width // 2
    bf = jnp.bfloat16
    scratch = []
    for make in (
        lambda n: (4, 4, 4, n, width),
        lambda n: (4, 4, 4, n, width),
        lambda n: (5, 2, 4, n, width),
        lambda n: (5, 2, 2, n, width),
        lambda n: (2, n, width),
        lambda n: (2, n, half),
    ):
        scratch += [pltpu.VMEM(make(n), bf) for _, n in PARTS]
    return pl.pallas_call(
        scatter_kernel,
        out_shape=(jax.ShapeDtypeStruct((rows, width), bf), jax.ShapeDtypeStruct(pg.shape[3:], pg.dtype)),
        in_specs=[pl.BlockSpec(memory_space=pl.ANY)] * 2,
        out_specs=[pl.BlockSpec(memory_space=pltpu.VMEM)] * 2,
        scratch_shapes=scratch + [
            pltpu.VMEM((4, 4) + pg.shape[3:], pg.dtype),
            pltpu.VMEM((4, 4) + pg.shape[3:], pg.dtype),
            pltpu.VMEM((2, 3, 4) + pg.shape[3:], pg.dtype),
            pltpu.VMEM((4,) + pg.shape[3:], pg.dtype),
            pltpu.SemaphoreType.DMA((10,)),
            pltpu.SemaphoreType.DMA((10,)),
            pltpu.SemaphoreType.DMA((3, 40)),
            pltpu.SemaphoreType.DMA((3, 40)),
            pltpu.SemaphoreType.DMA((4, 16)),
        ],
        compiler_params=pltpu.CompilerParams(collective_id=1, has_side_effects=True, vmem_limit_bytes=62 * 1024 * 1024),
    )(dense, pg)


def on_device(tokens, out_grad, router_probs, expert_ids, w_gate, w_up, w_down):
    toks, width = tokens.shape
    meta = jnp.concatenate([expert_ids.T.astype(jnp.float32), router_probs.T.astype(jnp.float32)], axis=0)
    gx, gy, gm = gather_all(tokens, out_grad, meta)
    flat = (32, 4, toks, width)
    dense, pg = expert_pass(gm.reshape((32,) + meta.shape), gx.reshape(flat), gy.reshape(flat), w_gate, w_up, w_down)
    token_grad, prob_grad = scatter_all(dense.reshape(gx.shape), pg.reshape((4, 4, 2) + pg.shape[1:]))
    return token_grad, prob_grad.T.astype(jnp.bfloat16)


def solution(mesh):
    return jax.shard_map(
        on_device,
        mesh=mesh,
        in_specs=(P("ctx", "tp"), P("ctx", "tp"), P("ctx", None), P("ctx", None), P("ctx", None, "tp"), P("ctx", None, "tp"), P("ctx", "tp", None)),
        out_specs=(P("ctx", "tp"), P("ctx", None)),
        check_vma=False,
    )
```

```python
import functools
import jax
import jax.numpy as jnp
from jax import lax
from jax.experimental import pallas as pl
from jax.experimental.pallas import tpu as pltpu
from jax.sharding import PartitionSpec as P

MESH = pl.DeviceIdType.MESH
ORDERS = (("x", "y", "z"), ("y", "z", "x"), ("z", "x", "y"))
SPLITS = (((0, 40), (40, 40), (80, 48)), ((0, 48), (48, 40), (88, 40)))


def my_place():
    ctx = lax.axis_index("ctx")
    return {"x": lax.axis_index("tp"), "y": ctx // 8, "z": (ctx // 2) % 4}, ctx % 2


def device_of(pos, core):
    return ((pos["y"] * 4 + pos["z"]) * 2 + core, pos["x"])


def shifted(pos, axis, by):
    other = dict(pos)
    other[axis] = (pos[axis] + by) % 4
    return other


def entry_barrier(pos, core):
    barrier = pltpu.get_barrier_semaphore()
    for axis in "xyz":
        for by in (1, 3):
            pl.semaphore_signal(barrier, inc=1, device_id=device_of(shifted(pos, axis, by), core), device_id_type=MESH)
    pl.semaphore_signal(barrier, inc=1, device_id=device_of(pos, 1 - core), device_id_type=MESH)
    pl.semaphore_wait(barrier, 7)


CAPS = 24
LAG = 8
PER_TICK = 4
PREP = 4


def pair_selectors(meta, first):
    top, toks = meta.shape[1] // 2, meta.shape[2]
    ids, probs = meta[:, :top].astype(jnp.int32), meta[:, top:]
    before = (lax.broadcasted_iota(jnp.int32, (toks, toks), 0) < lax.broadcasted_iota(jnp.int32, (toks, toks), 1)).astype(jnp.bfloat16)
    out = []
    for e in range(2):
        masks, hits, slots, weights = [], [], [], []
        for g in range(2):
            mask = (ids[g] == first + e).astype(jnp.float32)
            hit = jnp.sum(mask, axis=0, keepdims=True)
            slot = jnp.dot(jnp.broadcast_to(hit, (8, toks)).astype(jnp.bfloat16), before, preferred_element_type=jnp.float32)[0:1]
            masks.append(mask)
            hits.append(hit)
            slots.append(slot + float(CAPS * g))
            weights.append(jnp.sum(mask * probs[g], axis=0, keepdims=True))
        hit = jnp.concatenate(hits, axis=1)
        slot = jnp.concatenate(slots, axis=1)
        weight = jnp.concatenate(weights, axis=1)
        row = lax.broadcasted_iota(jnp.int32, (2 * CAPS, 2 * toks), 0)
        sel = jnp.where((row == slot.astype(jnp.int32)) & (hit > 0.5), 1.0, 0.0)
        out.append((sel, weight, masks))
    return out


def gather_kernel(both_ref, meta_ref, wg_hbm, wu_hbm, wd_hbm, g_ref, p_ref, pg_ref,
                  gm_ref, wgu, wd, xr, dr, rp, pw, pr, mixes, turned, stage, held, sums, back, grads,
                  send, recv, msend, mrecv, local, load_sem, out_sem):
    pos, core = my_place()
    first = lax.axis_index("ctx") * 2
    toks, width = both_ref.shape[1:]
    ff = wg_hbm.shape[2]
    loads = [pltpu.make_async_copy(src, dst, local.at[2 + n]) for n, (src, dst) in enumerate((
        (wg_hbm, wgu.at[:, :, pl.ds(0, ff)]), (wu_hbm, wgu.at[:, :, pl.ds(ff, ff)]), (wd_hbm, wd)))]
    entry_barrier(pos, core)
    started = []
    own = pltpu.make_async_copy(both_ref.at[core], g_ref.at[core, pos["y"], pos["z"], core, pos["x"]], local.at[0])
    own.start()
    swap = pltpu.make_async_remote_copy(
        src_ref=both_ref.at[1 - core], dst_ref=g_ref.at[1 - core, pos["y"], pos["z"], core, pos["x"]],
        send_sem=msend.at[7], recv_sem=mrecv.at[7], device_id=device_of(pos, 1 - core), device_id_type=MESH)
    swap.start()
    started.append(swap)
    own_meta = pltpu.make_async_copy(meta_ref, gm_ref.at[pos["y"], pos["z"], core], local.at[1])
    own_meta.start()

    def meta_program():
        def go(i, source, target, device):
            copy = pltpu.make_async_remote_copy(
                src_ref=source, dst_ref=target, send_sem=msend.at[i], recv_sem=mrecv.at[i],
                device_id=device, device_id_type=MESH)
            copy.start()
            started.append(copy)
            return copy

        here = gm_ref.at[pos["y"], pos["z"], core]
        one = go(0, meta_ref, here, device_of(shifted(pos, "y", 1), core))
        two = go(1, meta_ref, here, device_of(shifted(pos, "y", 3), core))
        yield
        one.wait_recv()
        back = gm_ref.at[shifted(pos, "y", 3)["y"], pos["z"], core]
        far = go(2, back, back, device_of(shifted(pos, "y", 1), core))
        two.wait_recv()
        yield
        far.wait_recv()
        own_meta.wait()
        here = gm_ref.at[:, pos["z"], core]
        one = go(3, here, here, device_of(shifted(pos, "z", 1), core))
        two = go(4, here, here, device_of(shifted(pos, "z", 3), core))
        yield
        one.wait_recv()
        back = gm_ref.at[:, shifted(pos, "z", 3)["z"], core]
        far = go(5, back, back, device_of(shifted(pos, "z", 1), core))
        two.wait_recv()
        yield
        far.wait_recv()
        mine = gm_ref.at[:, :, core]
        last = go(6, mine, mine, device_of(pos, 1 - core))
        yield
        last.wait_recv()

    def program(t, color):
        dst = g_ref.at[core]
        a, b, c = ORDERS[color]
        r0, rn = SPLITS[t][color]
        rows = pl.ds(r0, rn)

        def slot(at, whole, part=None):
            index = {k: (slice(None) if k in whole else at[k]) for k in "xyz"}
            some = rows
            if part is not None and whole:
                index[a] = pl.ds(2 * part, 2)
            elif part is not None:
                some = pl.ds(r0, 24) if part == 0 else pl.ds(r0 + 24, rn - 24)
            return dst.at[index["y"], index["z"], t, index["x"], some]

        def go(i, source, target, device):
            copy = pltpu.make_async_remote_copy(
                src_ref=source, dst_ref=target, send_sem=send.at[t, color, i],
                recv_sem=recv.at[t, color, i], device_id=device, device_id_type=MESH)
            copy.start()
            started.append(copy)
            return copy

        def block_out(i, at, whole, axis, source=None):
            here = slot(at, whole)
            from_ref = here if source is None else source
            return (go(i, from_ref, here, device_of(shifted(pos, axis, 1), core)),
                    go(i + 1, from_ref, here, device_of(shifted(pos, axis, 3), core)))

        def relay(i, at, whole, axis, pair):
            pair[0].wait_recv()
            piece = slot(shifted(at, axis, 3), whole, 0)
            one = go(i + 2, piece, piece, device_of(shifted(pos, axis, 1), core))
            pair[1].wait_recv()
            piece = slot(shifted(at, axis, 1), whole, 1)
            two = go(i + 3, piece, piece, device_of(shifted(pos, axis, 3), core))
            return one, two

        sib_count = [0]
        sibs = []

        def sibling(at):
            piece = slot(at, (a,))
            sibs.append(go(24 + sib_count[0], piece, piece, device_of(pos, 1 - core)))
            sib_count[0] += 1

        pair = block_out(0, pos, (), a)
        yield
        far = relay(0, pos, (), a, pair)
        yield
        for f in far:
            f.wait_recv()
        pair = block_out(4, pos, (a,), b)
        lasts = [(8, pos, block_out(8, pos, (a,), c))]
        sibling(pos)
        yield
        far = relay(4, pos, (a,), b, pair)
        for n, by in ((12, 3), (16, 1)):
            at = shifted(pos, b, by)
            lasts.append((n, at, block_out(n, at, (a,), c)))
            sibling(at)
        yield
        for f in far:
            f.wait_recv()
        at = shifted(pos, b, 2)
        lasts.append((20, at, block_out(20, at, (a,), c)))
        sibling(at)
        fars = []
        for n, at, pair in lasts:
            yield
            fars.append((at, relay(n, at, (a,), c, pair)))
            sibling(shifted(at, c, 3))
            sibling(shifted(at, c, 1))
            if len(fars) > 1:
                at2, far = fars[-2]
                for f in far:
                    f.wait_recv()
                sibling(shifted(at2, c, 2))
        yield
        at2, far = fars[-1]
        for f in far:
            f.wait_recv()
        sibling(shifted(at2, c, 2))
        yield
        for s in sibs:
            s.wait_recv()


    pairs = [(p // 2, 2 * (p % 2)) for p in range(8)]

    def prepare():
        for w in range(2):
            for p, (y, z) in enumerate(pairs):
                chosen = pair_selectors(gm_ref[y, pl.ds(z, 2), w], first)
                mix = jnp.concatenate([c[0] for c in chosen], axis=0)
                mixes[w, p] = mix.astype(jnp.bfloat16)
                turned[w, p] = mix.T.astype(jnp.bfloat16)
                for e in range(2):
                    col = jnp.sum(chosen[e][0] * chosen[e][1], axis=1, keepdims=True)
                    pw[w, e, pl.ds(p * 2 * CAPS, 2 * CAPS), :] = jnp.broadcast_to(col, (2 * CAPS, 128))
                yield

    def experts(w):
        copies = {}

        def fetch(n):
            y, z = pairs[n // 2]
            copies[n] = pltpu.make_async_copy(g_ref.at[n % 2, y, pl.ds(z, 2), w], stage.at[n % 2], load_sem.at[n % 2])
            copies[n].start()

        fetch(0)
        fetch(1)
        for p, (y, z) in enumerate(pairs):
            at = pl.ds(p * 2 * CAPS, 2 * CAPS)
            for t, dst in enumerate((xr, dr)):
                n = 2 * p + t
                copies[n].wait()

                def pick(q, carry):
                    two = stage[t, :, q].reshape(2 * toks, width)
                    rows = jnp.dot(mixes[w, p], two, preferred_element_type=jnp.float32).astype(jnp.bfloat16)
                    cols = pl.ds(pl.multiple_of(q * width, width), width)
                    for e in range(2):
                        dst[e, at, cols] = rows[e * 2 * CAPS:(e + 1) * 2 * CAPS]
                    return carry
                lax.fori_loop(0, 4, pick, 0)
                if n + 2 < 16:
                    fetch(n + 2)
            yield
        if w == 0:
            for load in loads:
                load.wait()
        for e in range(2):
            def product(into, rows, weight, dims):
                into[...] = jnp.zeros_like(into)

                def body(k, carry):
                    cols = pl.ds(pl.multiple_of(k * width, width), width)
                    other = weight[e, cols, :] if dims == 0 else weight[e, :, cols]
                    into[...] += lax.dot_general(rows[e, :, cols], other, (((1,), (dims,)), ((), ())), preferred_element_type=jnp.float32)
                    return carry
                lax.fori_loop(0, 4, body, 0)

            product(sums, xr, wgu, 0)
            yield
            product(back, dr, wd, 1)
            yield
            gate, ups, backs = sums[:, :ff], sums[:, ff:], back[...]
            sig = jax.nn.sigmoid(gate)
            gated = gate * sig
            pr[e] = jnp.broadcast_to(jnp.sum(gated * ups * backs, axis=1, keepdims=True), pr.shape[1:])
            scaled = pw[w, e, :, 0:1] * backs
            grads[:, :ff] = (scaled * ups * sig * (1.0 + gate * (1.0 - sig))).astype(jnp.bfloat16)
            grads[:, ff:] = (scaled * gated).astype(jnp.bfloat16)

            def spread(k, carry):
                cols = pl.ds(pl.multiple_of(k * width, width), width)
                dims = (((1,), (1,)), ((), ()))
                part = lax.dot_general(grads[...], wgu[e, cols, :], dims, preferred_element_type=jnp.float32)
                rp[e, :, cols] = part.astype(jnp.bfloat16)
                return carry
            lax.fori_loop(0, 2, spread, 0)
            yield
            lax.fori_loop(2, 4, spread, 0)
            yield
        outs = []
        for p, (y, z) in enumerate(pairs):
            at = pl.ds(p * 2 * CAPS, 2 * CAPS)
            if p >= 2:
                outs[p - 2].wait()
            slot = p % 2

            def emit(q, carry):
                cols = pl.ds(pl.multiple_of(q * width, width), width)
                rows = jnp.concatenate([rp[e, at, cols] for e in range(2)], axis=0)
                dense = jnp.dot(turned[w, p], rows, preferred_element_type=jnp.float32).astype(jnp.bfloat16)
                for g in range(2):
                    held[slot, g, q] = dense[g * toks:(g + 1) * toks]
                return carry
            lax.fori_loop(0, 4, emit, 0)
            copy = pltpu.make_async_copy(held.at[slot], p_ref.at[y, pl.ds(z, 2), w], out_sem.at[slot])
            copy.start()
            outs.append(copy)
            total = [0.0, 0.0]
            for e in range(2):
                sel = mixes[w, p, pl.ds(e * 2 * CAPS, 2 * CAPS)].astype(jnp.float32)
                value = jnp.sum(sel * pr[e, at, 0:1], axis=0, keepdims=True)
                for g in range(2):
                    mask = (gm_ref[y, z + g, w, :pg_ref.shape[3]].astype(jnp.int32) == first + e).astype(jnp.float32)
                    total[g] = total[g] + mask * value[:, g * toks:(g + 1) * toks]
            for g in range(2):
                pg_ref[y, z + g, w] = total[g]
            yield
        for copy in outs[-2:]:
            copy.wait()

    own.wait()
    swap.wait_recv()
    gathers = [[program(w, color) for color in range(3)] for w in range(2)]
    meta_run = [meta_program()]

    def advance(group):
        group[:] = [g for g in group if next(g, "done") != "done"]

    tick = 0
    prep = [prepare()]
    while gathers[0]:
        for _ in range(0 if meta_run else PREP):
            advance(prep)
        advance(meta_run)
        advance(gathers[0])
        if tick == 3:
            for load in loads:
                load.start()
        if tick >= LAG:
            advance(gathers[1])
        tick += 1
    while prep:
        advance(prep)
    work = [experts(0)]
    while gathers[1] or work:
        for _ in range(PER_TICK if gathers[1] else 100):
            advance(work)
        advance(gathers[1])
    work = [experts(1)]
    while work:
        advance(work)
    for s in started:
        s.wait_send()


def gather_all(both, meta, wg, wu, wd):
    toks, width = both.shape[1:]
    bf, f32 = jnp.bfloat16, jnp.float32
    depth, ff = wg.shape[1:]
    rows = 16 * CAPS
    top = meta.shape[0] // 2
    any_, vm = pl.BlockSpec(memory_space=pl.ANY), pl.BlockSpec(memory_space=pltpu.VMEM)
    return pl.pallas_call(
        gather_kernel,
        out_shape=(
            jax.ShapeDtypeStruct((2, 4, 4, 2, 4, toks, width), bf),
            jax.ShapeDtypeStruct((4, 4, 2, 4, toks, width), bf),
            jax.ShapeDtypeStruct((4, 4, 2, top, toks), f32),
        ),
        in_specs=[vm, vm, any_, any_, any_],
        out_specs=[any_, any_, vm],
        scratch_shapes=[
            pltpu.VMEM((4, 4, 2) + meta.shape, meta.dtype),
            pltpu.VMEM((2, depth, 2 * ff), bf), pltpu.VMEM(wd.shape, bf),
            pltpu.VMEM((2, rows, depth), bf), pltpu.VMEM((2, rows, depth), bf), pltpu.VMEM((2, rows, depth), bf),
            pltpu.VMEM((2, 2, rows, 128), f32), pltpu.VMEM((2, rows, 128), f32),
            pltpu.VMEM((2, 8, 4 * CAPS, 2 * toks), bf), pltpu.VMEM((2, 8, 2 * toks, 4 * CAPS), bf),
            pltpu.VMEM((2, 2, 4, toks, width), bf), pltpu.VMEM((2, 2, 4, toks, width), bf),
            pltpu.VMEM((rows, 2 * ff), f32), pltpu.VMEM((rows, ff), f32), pltpu.VMEM((rows, 2 * ff), bf),
            pltpu.SemaphoreType.DMA((2, 3, 40)), pltpu.SemaphoreType.DMA((2, 3, 40)),
            pltpu.SemaphoreType.DMA((8,)), pltpu.SemaphoreType.DMA((8,)),
            pltpu.SemaphoreType.DMA((5,)), pltpu.SemaphoreType.DMA((2,)), pltpu.SemaphoreType.DMA((2,)),
        ],
        compiler_params=pltpu.CompilerParams(collective_id=0, has_side_effects=True, vmem_limit_bytes=62 * 1024 * 1024),
    )(both, meta, wg, wu, wd)

PARTS = ((0, 48), (48, 48), (96, 32))


def scatter_kernel(p_ref, pg_ref, out_ref, prob_ref, *scratch):
    accs, sibs, fulls, parts, lone_full, lone_part = (scratch[3 * i:3 * i + 3] for i in range(6))
    pacc, psib, pring, pall, psend, precv, send, recv, local = scratch[18:]
    pos, core = my_place()
    entry_barrier(pos, core)
    width = out_ref.shape[1]
    half = width // 2
    cuts = (pl.ds(0, half), pl.ds(half, half))
    started = []

    def go(color, i, source, target, device):
        copy = pltpu.make_async_remote_copy(
            src_ref=source, dst_ref=target, send_sem=send.at[color, i],
            recv_sem=recv.at[color, i], device_id=device, device_id_type=MESH)
        copy.start()
        started.append(copy)
        return copy

    def prob_program():
        def go(i, source, target, device):
            copy = pltpu.make_async_remote_copy(
                src_ref=source, dst_ref=target, send_sem=psend.at[i], recv_sem=precv.at[i],
                device_id=device, device_id_type=MESH)
            copy.start()
            started.append(copy)
            return copy

        load = pltpu.make_async_copy(pg_ref.at[:, :, core], pacc, local.at[3, 0])
        load.start()
        push = go(0, pg_ref.at[:, :, 1 - core], psib, device_of(pos, 1 - core))
        yield
        load.wait()
        push.wait_recv()
        for i in range(4):
            pacc[i] = pacc[i] + psib[i]
        n = 1
        for stage, axis in enumerate("zy"):
            def spot(by):
                at = shifted(pos, axis, by)
                return (slice(None), at["z"]) if axis == "z" else (pl.ds(at["y"], 1), at["z"])
            size = 4 if axis == "z" else 1
            ring = [pring.at[stage, i, pl.ds(0, size)] for i in range(3)]
            plus, minus = device_of(shifted(pos, axis, 1), core), device_of(shifted(pos, axis, 3), core)
            far = go(n, pacc.at[spot(2)], ring[0], plus)
            yield
            far.wait_recv()
            pacc[spot(1)] = pacc[spot(1)] + ring[0][...]
            one = go(n + 1, pacc.at[spot(1)], ring[1], plus)
            two = go(n + 2, pacc.at[spot(3)], ring[2], minus)
            yield
            one.wait_recv()
            two.wait_recv()
            pacc[spot(0)] = pacc[spot(0)] + ring[1][...] + ring[2][...]
            n += 3
        pall[pos["x"]] = pacc[pos["y"], pos["z"]]
        here = pall.at[pos["x"]]
        one = go(n, here, here, device_of(shifted(pos, "x", 1), core))
        two = go(n + 1, here, here, device_of(shifted(pos, "x", 3), core))
        yield
        one.wait_recv()
        back = pall.at[shifted(pos, "x", 3)["x"]]
        far = go(n + 2, back, back, device_of(shifted(pos, "x", 1), core))
        two.wait_recv()
        yield
        far.wait_recv()
        prob_ref[...] = pall[0] + pall[1] + pall[2] + pall[3]

    def program(color):
        a, b, c = ORDERS[color]
        rows = pl.ds(*PARTS[color])
        acc, sib = accs[color], sibs[color]

        def where(at, whole):
            index = {k: (slice(None) if k in whole else at[k]) for k in "xyz"}
            return index["y"], index["z"], index["x"]

        def line(at, part=None):
            index = dict(zip("yzx", where(at, (a,))))
            if part is not None:
                index[a] = pl.ds(2 * part, 2)
            return acc.at[index["y"], index["z"], index["x"]]

        def add_line(at, part, other):
            low, high = (0, 4) if part is None else (2 * part, 2 * part + 2)

            def body(i, carry):
                mine = dict(at)
                mine[a] = i
                spot = where(mine, ())
                acc[spot] = acc[spot] + other(i - low)
                return carry
            lax.fori_loop(low, high, body, 0)

        loads = {}
        order = (2, 1, 3, 0)
        count = 0
        for j in order:
            for k in order:
                at = shifted(shifted(pos, b, j), c, k)
                y, z, x = where(at, (a,))
                load = pltpu.make_async_copy(p_ref.at[y, z, core, x, rows], line(at), local.at[color, count])
                load.start()
                push = go(color, 24 + count, p_ref.at[y, z, 1 - core, x, rows], sib.at[y, z, x], device_of(pos, 1 - core))
                loads[j, k] = (at, load, push)
                count += 1
            yield

        def merge(j, k):
            at, load, push = loads[j, k]
            load.wait()
            push.wait_recv()

            def other(i):
                mine = dict(at)
                mine[a] = i
                return sib[where(mine, ())]
            add_line(at, None, other)

        def first(n, axis, unit):
            return (go(color, n * 4, unit(2, 0), parts[color].at[n, 0], device_of(shifted(pos, axis, 1), core)),
                    go(color, n * 4 + 1, unit(2, 1), parts[color].at[n, 1], device_of(shifted(pos, axis, 3), core)))

        def second(n, axis, unit, add, halves):
            sent = []
            for side, by in ((0, 1), (1, 3)):
                halves[side].wait_recv()
                add(by, side, lambda i, side=side: parts[color][n, side, i])
                sent.append(go(color, n * 4 + 2 + side, unit(by, None), fulls[color].at[n, side],
                               device_of(shifted(pos, axis, by), core)))
            return sent

        def third(n, add, sent):
            for side in range(2):
                sent[side].wait_recv()
                add(0, None, lambda i, side=side: fulls[color][n, side, i])

        def last_unit(j):
            return (lambda k, cols: line(shifted(shifted(pos, b, j), c, k), cols),
                    lambda k, cols, other: add_line(shifted(shifted(pos, b, j), c, k), cols, other))

        halves, sents = {}, {}

        def stage_a(n):
            merge(order[n], 2)
            halves[n] = first(n, c, last_unit(order[n])[0])

        def stage_b(n):
            merge(order[n], 1)
            merge(order[n], 3)
            unit, add = last_unit(order[n])
            sents[n] = second(n, c, unit, add, halves[n])

        def stage_c(n):
            merge(order[n], 0)
            third(n, last_unit(order[n])[1], sents[n])

        mid_unit = lambda k, cols: line(shifted(pos, b, k), cols)
        mid_add = lambda k, cols, other: add_line(shifted(pos, b, k), cols, other)
        stage_a(0)
        yield
        stage_a(1)
        yield
        stage_b(0)
        yield
        stage_a(2)
        yield
        stage_b(1)
        yield
        stage_c(0)
        mid_halves = first(4, b, mid_unit)
        yield
        stage_a(3)
        yield
        stage_b(2)
        yield
        stage_c(1)
        yield
        stage_b(3)
        yield
        stage_c(2)
        mid_sent = second(4, b, mid_unit, mid_add, mid_halves)
        yield
        stage_c(3)
        third(4, mid_add, mid_sent)
        yield

        def one(at, cols=slice(None)):
            return acc.at[(*where(at, ()), slice(None), cols)]

        def add_one(by, cols, other):
            spot = (*where(shifted(pos, a, by), ()), slice(None), cols)
            acc[spot] = acc[spot] + other

        tail = [go(color, 20, one(shifted(pos, a, 2), cuts[0]), lone_part[color].at[0], device_of(shifted(pos, a, 1), core)),
                go(color, 21, one(shifted(pos, a, 2), cuts[1]), lone_part[color].at[1], device_of(shifted(pos, a, 3), core))]
        yield
        sent = []
        for side, by in ((0, 1), (1, 3)):
            tail[side].wait_recv()
            add_one(by, cuts[side], lone_part[color][side])
            sent.append(go(color, 22 + side, one(shifted(pos, a, by)), lone_full[color].at[side], device_of(shifted(pos, a, by), core)))
        yield
        for side in range(2):
            sent[side].wait_recv()
            add_one(0, slice(None), lone_full[color][side])
        out_ref[rows, :] = acc[where(pos, ())]

    live = [prob_program()] + [program(color) for color in range(3)]
    while live:
        still = []
        for prog in live:
            try:
                next(prog)
                still.append(prog)
            except StopIteration:
                pass
        live = still
    for s in started:
        s.wait_send()


def scatter_all(dense, pg):
    rows, width = dense.shape[-2:]
    half = width // 2
    bf = jnp.bfloat16
    scratch = []
    for make in (
        lambda n: (4, 4, 4, n, width),
        lambda n: (4, 4, 4, n, width),
        lambda n: (5, 2, 4, n, width),
        lambda n: (5, 2, 2, n, width),
        lambda n: (2, n, width),
        lambda n: (2, n, half),
    ):
        scratch += [pltpu.VMEM(make(n), bf) for _, n in PARTS]
    return pl.pallas_call(
        scatter_kernel,
        out_shape=(jax.ShapeDtypeStruct((rows, width), bf), jax.ShapeDtypeStruct(pg.shape[3:], pg.dtype)),
        in_specs=[pl.BlockSpec(memory_space=pl.ANY)] * 2,
        out_specs=[pl.BlockSpec(memory_space=pltpu.VMEM)] * 2,
        scratch_shapes=scratch + [
            pltpu.VMEM((4, 4) + pg.shape[3:], pg.dtype),
            pltpu.VMEM((4, 4) + pg.shape[3:], pg.dtype),
            pltpu.VMEM((2, 3, 4) + pg.shape[3:], pg.dtype),
            pltpu.VMEM((4,) + pg.shape[3:], pg.dtype),
            pltpu.SemaphoreType.DMA((10,)),
            pltpu.SemaphoreType.DMA((10,)),
            pltpu.SemaphoreType.DMA((3, 40)),
            pltpu.SemaphoreType.DMA((3, 40)),
            pltpu.SemaphoreType.DMA((4, 16)),
        ],
        compiler_params=pltpu.CompilerParams(collective_id=1, has_side_effects=True, vmem_limit_bytes=62 * 1024 * 1024),
    )(dense, pg)


def on_device(tokens, out_grad, router_probs, expert_ids, w_gate, w_up, w_down):
    toks, width = tokens.shape
    meta = jnp.concatenate([expert_ids.T.astype(jnp.float32), router_probs.T.astype(jnp.float32)], axis=0)
    both = jnp.stack([tokens, out_grad])
    _, dense, pg = gather_all(both, meta, w_gate, w_up, w_down)
    token_grad, prob_grad = scatter_all(dense, pg)
    return token_grad, prob_grad.T.astype(jnp.bfloat16)


def solution(mesh):
    return jax.shard_map(
        on_device,
        mesh=mesh,
        in_specs=(P("ctx", "tp"), P("ctx", "tp"), P("ctx", None), P("ctx", None), P("ctx", None, "tp"), P("ctx", None, "tp"), P("ctx", "tp", None)),
        out_specs=(P("ctx", "tp"), P("ctx", None)),
        check_vma=False,
    )
```
